512 devices in a mesh: dp: 16 (over y, core), expert: 32 (over x, z).
Axes of the slice: x: 4, y: 8, z: 8, core: 2. Of those that a mesh axis runs over, the one named last changes fastest.
Arguments:
- attention: bfloat16 [65536, 1536], P(('dp', 'expert')), may hold values from -6 to 6
- residual: bfloat16 [65536, 1536], P(('dp', 'expert')), may hold values from -6 to 6
- out_weight: bfloat16 [1536, 1536], P(('dp', 'expert')), may hold values from -0.15625 to 0.15625
- gate_weight: bfloat16 [32, 1536, 512], P('expert', 'dp'), may hold values from -0.15625 to 0.15625
- up_weight: bfloat16 [32, 1536, 512], P('expert', 'dp'), may hold values from -0.15625 to 0.15625
- down_weight: bfloat16 [32, 512, 1536], P('expert'), may hold values from -0.25 to 0.25
- routes: int32 [65536, 8], P(('dp', 'expert')), may hold values from 0 to 31, all different within a row; in each aligned block of 128 rows (0 to 127, 128 to 255, ...) at most 40 rows name the same one
- router_scores: float32 [65536, 8], P(('dp', 'expert')), may hold values from 0.05 to 1
- norm_gain: float32 [1536], replicated, may hold values from 0.5 to 1.5
Outputs:
- normed: bfloat16 [65536, 1536], P(('dp', 'expert'))
The draws below stay inside these ranges and needn't reach their ends.
Inputs may be any that keep to these rules, and one draw needn't show every extreme that they name: `routes`: in each aligned block of 128 rows (the rows of one device) no expert is named by more than 40 rows, a bound that some block reaches; a row names 8 different experts.
All inputs are finite; a program needn't handle non-finite values.
Results may differ from the reference program's by a relative error of at most 0.0053.
Values may be sent and summed in bfloat16 or wider, within the bound.
A program may use at most 64 MiB of HBM per device.

```python
import math
import jax
import jax.numpy as jnp
import numpy as np
from jax import lax

D = 1536
FFH = 512
TOPK = 8
TOK_DEV = 128
EXPERTS = 32
CAP = 40
TOKENS = 65536


def block_levels(rng, extent, split, least, largest):
    def one(dim, parts):
        draws = jax.random.uniform(jax.random.fold_in(jax.random.fold_in(rng, 6), dim), (parts,), jnp.float32, least / len(split), largest / len(split))
        return jnp.repeat(jnp.exp(draws), extent[dim] // parts).reshape((-1,) + (1,) * (len(extent) - dim - 1))

    level = one(*split[0])
    for cut in split[1:]:
        level = level * one(*cut)
    return level


def routed_block(rng, own, number, rows, amount, top, bound, lean):
    order = jax.random.permutation(rng, amount)
    heavy_load, common = shares(amount, rows * top, bound, lean, True), shares(amount, rows * top, bound, lean, False)
    places = jnp.arange(amount)

    def named(lengths, offset_by):
        used = int((lengths > 0).sum())
        fixed = max(1, used // 4)
        shifted = fixed + (places - fixed + offset_by * (used - fixed)) % max(1, amount - fixed)
        return jnp.zeros((amount,), jnp.int32).at[order[jnp.where(places < fixed, places, shifted)]].set(jnp.asarray(lengths, jnp.int32))

    lengths = jnp.where(number % 4 == 0, named(heavy_load, number // 4), named(common, number - number // 4 - 1))
    mixed = jax.random.permutation(jax.random.fold_in(own, 3), amount)
    donor, taker = mixed[0:amount // 2 * 2:2], mixed[1:amount // 2 * 2:2]
    room = jnp.minimum(lengths[donor] - 1, bound - lengths[taker]) // 2
    room = jnp.where((donor == order[0]) | (taker == order[0]) | (lengths[taker] == 0), 0, jnp.maximum(room, 0))
    shifted = jax.random.randint(jax.random.fold_in(own, 4), (amount // 2,), 0, 1 << 20) % (room + 1)
    lengths = lengths.at[donor].add(-shifted).at[taker].add(shifted)
    members = jnp.searchsorted(jnp.cumsum(lengths), jnp.arange(rows * top), side="right").astype(jnp.int32)
    grid = members.reshape(top, rows).T
    grid = grid[jax.random.permutation(jax.random.fold_in(own, 1), rows)]
    offset_by = jax.random.randint(jax.random.fold_in(own, 2), (rows, 1), 0, top)
    return jnp.take_along_axis(grid, (jnp.arange(top)[None, :] + offset_by) % top, axis=1)


def shares(amount, total, limit, skew, full):
    weights = [(1 << 20) // math.isqrt(grade ** skew) + 1 for grade in range(1, amount + 1)]
    largest = limit if full else min(limit, max(-(-total // amount), total * weights[0] // sum(weights)))
    least = 1 if total - largest >= amount - 1 else 0
    counts, surplus = [largest] + [least] * (amount - 1), total - largest - least * (amount - 1)
    while surplus > 0:
        movable = [i for i in range(1, amount) if counts[i] < largest] or [i for i in range(1, amount) if counts[i] < limit]
        whole, budget = sum([weights[i] for i in movable]), surplus
        for i in movable:
            addition = min(limit - counts[i], max(1, budget * weights[i] // whole), surplus)
            counts[i] = counts[i] + addition
            surplus = surplus - addition
    return np.array(counts)


def bell_draw(rng, dims, scale, limit, pieces=(), held_as=jnp.bfloat16):
    factor_of = block_levels(rng, dims, pieces, -0.22, 0.18) if pieces else 1.0
    result = jax.random.normal(rng, dims, jnp.float32) * scale * factor_of
    return jnp.minimum(jnp.maximum(result, -limit), limit).astype(held_as)


def setup_inputs(seed: int = 0) -> dict:
    streams_of = jax.random.split(jax.random.key(seed), 10)
    attention = bell_draw(streams_of[0], (TOKENS, D), 1.0, 6.0, ((0, 512),))
    residual = bell_draw(streams_of[1], (TOKENS, D), 1.0, 6.0, ((0, 512),))
    out_weight = bell_draw(streams_of[2], (D, D), D ** -0.5, 0.15625, ((0, 512),))
    gate_weight = bell_draw(streams_of[3], (EXPERTS, D, FFH), D ** -0.5, 0.15625, ((0, 32), (1, 16)))
    up_weight = bell_draw(streams_of[4], (EXPERTS, D, FFH), D ** -0.5, 0.15625, ((0, 32), (1, 16)))
    down_weight = bell_draw(streams_of[5], (EXPERTS, FFH, D), FFH ** -0.5, 0.25, ((0, 32),))
    routes_keys = jax.random.split(jax.random.fold_in(streams_of[6], 1), TOKENS // TOK_DEV)
    routes_turns = jax.random.permutation(jax.random.fold_in(streams_of[6], 3), TOKENS // TOK_DEV)
    routes = jax.vmap(lambda own, number: routed_block(jax.random.fold_in(streams_of[6], 2), own, number, TOK_DEV, EXPERTS, TOPK, CAP, 2))(routes_keys, routes_turns).reshape((TOKENS, TOPK))
    router_scores = jnp.clip(jnp.exp(math.log(1.0) - 2.9957323 * jax.random.uniform(streams_of[7], (TOKENS, TOPK), jnp.float32) ** block_levels(streams_of[7], (TOKENS, TOPK), ((0, 512),), -0.2, 0.2)), 0.05, 1.0)
    norm_gain = jnp.clip(1.0 + 0.1 * jax.random.normal(streams_of[8], (D,), jnp.float32), 0.5, 1.5)
    return {"attention": attention, "residual": residual, "out_weight": out_weight, "gate_weight": gate_weight, "up_weight": up_weight, "down_weight": down_weight, "routes": routes, "router_scores": router_scores, "norm_gain": norm_gain}


def reference(attention, residual, out_weight, gate_weight, up_weight, down_weight, routes, router_scores, norm_gain):
    projected = jnp.dot(attention, out_weight, preferred_element_type=jnp.float32)
    stream = (residual.astype(jnp.float32) + projected).astype(jnp.bfloat16)
    groups = TOKENS // TOK_DEV
    pairs = routes.reshape(groups, TOK_DEV * TOPK).astype(jnp.int32)
    onehot = (pairs[:, :, None] == jnp.arange(EXPERTS, dtype=jnp.int32)[None, None, :]).astype(jnp.int32)
    earlier = jnp.cumsum(onehot, axis=1) - onehot
    position = lax.optimization_barrier(jnp.sum(earlier * onehot, axis=2)).astype(jnp.int32)
    group_index = jnp.arange(groups, dtype=jnp.int32)[:, None]
    target = pairs * (groups * CAP) + group_index * CAP + position
    token_index = group_index * TOK_DEV + jnp.arange(TOK_DEV * TOPK, dtype=jnp.int32)[None, :] // TOPK
    combine = router_scores / lax.optimization_barrier(jnp.sum(router_scores, axis=1, keepdims=True))
    table = jnp.full((EXPERTS * groups * CAP,), TOKENS, jnp.int32).at[target.reshape(-1)].set(token_index.reshape(-1))
    table = table.reshape(EXPERTS, groups * CAP)
    weight_table = jnp.zeros((EXPERTS * groups * CAP,), jnp.float32).at[target.reshape(-1)].set(combine.reshape(-1))
    weight_table = weight_table.reshape(EXPERTS, groups * CAP)
    padded = jnp.concatenate([stream, jnp.zeros((1, D), jnp.bfloat16)], axis=0)

    def one_expert(mixture, items):
        indices, weights, gate_mat, up_mat, down_mat = items
        rows_in = padded[indices]
        gate_act = jnp.dot(rows_in, gate_mat, preferred_element_type=jnp.float32)
        up_act = jnp.dot(rows_in, up_mat, preferred_element_type=jnp.float32)
        expert_hidden = (jax.nn.silu(gate_act) * up_act).astype(jnp.bfloat16)
        expert_out = jnp.dot(expert_hidden, down_mat, preferred_element_type=jnp.float32).astype(jnp.bfloat16)
        mixture = mixture.at[indices].add(weights[:, None] * expert_out.astype(jnp.float32))
        return (mixture, None)
    start_mix = jnp.zeros((TOKENS + 1, D), jnp.float32)
    mixture, unused = lax.scan(one_expert, start_mix, (table, weight_table, gate_weight, up_weight, down_weight))
    total = stream.astype(jnp.float32) + mixture[:TOKENS]
    scale = lax.rsqrt(lax.optimization_barrier(jnp.mean(total * total, axis=1, keepdims=True)) + 1e-06)
    return (total * scale * norm_gain[None, :]).astype(jnp.bfloat16)
```

```python
import jax
import jax.numpy as jnp
import numpy as np
from jax import lax
from jax.experimental import pallas as pl
from jax.experimental.pallas import tpu as pltpu
from jax.sharding import PartitionSpec as P

NX, NY, NZ = 4, 8, 8
CAP = 40
PAIR = 2 * CAP
SLOT = {0: 0, 4: 1, 1: 2, -1: 3, 2: 4, -2: 5, 3: 6, -3: 7}


def rel_slot(r):
    r = r % NZ
    return SLOT[r if r <= 4 else r - NZ]


class Net:
    def __init__(self, send_sems, recv_sems):
        self.ss, self.rs, self.count, self.sent = send_sems, recv_sems, 0, []

    def send(self, src, dst, device):
        i = self.count
        self.count += 1
        copy = pltpu.make_async_remote_copy(
            src_ref=src, dst_ref=dst, send_sem=self.ss.at[i], recv_sem=self.rs.at[i],
            device_id=device, device_id_type=pl.DeviceIdType.MESH,
        )
        copy.start()
        self.sent.append(copy)
        return i

    def arrive(self, i, region, device):
        pltpu.make_async_remote_copy(
            src_ref=region, dst_ref=region, send_sem=self.ss.at[i], recv_sem=self.rs.at[i],
            device_id=device, device_id_type=pl.DeviceIdType.MESH,
        ).wait_recv()

    def drain(self):
        for copy in self.sent:
            copy.wait_send()


N_COPIES = 140


def kernel(
    att, res, ow, gate, up, down, routes_t, scores_t, gain, kperm,
    out,
    s1, s1f, OW, G, U, DN, tok, meta, tab, sel, wrow, X, Y, SB, RB, part, aperm,
    send_sems, recv_sems, loc_sems,
):
    f32, bf16 = jnp.float32, jnp.bfloat16
    T, F = att.shape
    H = gate.shape[1]
    rows = gate.shape[0]
    dp, ex = lax.axis_index("dp"), lax.axis_index("expert")
    y, c = lax.div(dp, 2), lax.rem(dp, 2)
    x, z = lax.div(ex, NZ), lax.rem(ex, NZ)

    def md(a, n):
        return lax.rem(a + 2 * n, n)

    def dev(dx=0, dy=0, dz=0, other=False):
        cc = 1 - c if other else c
        return (md(y + dy, NY) * 2 + cc, md(x + dx, NX) * NZ + md(z + dz, NZ))

    partner = dev(other=True)
    barrier = pltpu.get_barrier_semaphore()
    peers = (
        [dev(dx=d) for d in range(1, NX)] + [dev(dy=d) for d in range(1, NY)]
        + [dev(dz=d) for d in range(1, NZ)] + [partner]
    )
    for p in peers:
        pl.semaphore_signal(barrier, inc=1, device_id=p, device_id_type=pl.DeviceIdType.MESH)
    pl.semaphore_wait(barrier, len(peers))

    net = Net(send_sems, recv_sems)

    def local(k, src, dst):
        copy = pltpu.make_async_copy(src, dst, loc_sems.at[k])
        copy.start()
        return copy

    own_ow = local(0, ow, s1.at[y, x])
    s1x = [(net.send(ow, s1.at[y, x], dev(dx=d)), d) for d in range(1, NX)]

    def wslice(W, e, yb, cc):
        return W.at[e, pl.ds(pl.multiple_of((yb * 2 + cc) * rows, 8), rows)]

    half = H // 2
    my_half = pl.ds(pl.multiple_of(c * half, 8), half)
    own_g = local(1, gate, wslice(G, x, y, c))
    own_u = local(2, up, wslice(U, x, y, c))
    own_d = local(3, down, DN.at[x])
    gux = []
    for d in (1, 3, 2):
        for src, W in ((gate, G), (up, U)):
            gux.append((net.send(src, wslice(W, x, y, c), dev(dx=d)), W, d))

    r8 = lax.broadcasted_iota(jnp.int32, (NZ * 8, T), 0)
    expert = (r8 % 4) * NZ + r8 // 8
    scores = scores_t[...]
    combine = scores / jnp.sum(scores, axis=0, keepdims=True)
    member = jnp.zeros((NZ * 8, T), f32)
    weight = jnp.zeros((NZ * 8, T), f32)
    for k in range(routes_t.shape[0]):
        hit = routes_t[k : k + 1, :] == expert
        member = member + jnp.where(hit, 1.0, 0.0)
        weight = weight + jnp.where(hit, combine[k : k + 1, :], 0.0)
    before = lax.broadcasted_iota(jnp.int32, (T, T), 0) < lax.broadcasted_iota(jnp.int32, (T, T), 1)
    place = jnp.dot(member.astype(bf16), jnp.where(before, 1.0, 0.0).astype(bf16), preferred_element_type=f32)
    table = jnp.where(r8 % 8 < 4, jnp.where(member > 0.5, place, -1000.0), weight)
    tab[...] = table.reshape(NZ, 8, T)
    meta[0] = tab[z]
    metas = []
    for d in range(1, NZ):
        metas.append((net.send(tab.at[md(z + d, NZ)], meta.at[rel_slot(-d)], dev(dz=d)), d))

    own_ow.wait()
    for i, d in s1x:
        net.arrive(i, s1.at[y, md(x - d, NX)], dev(dx=-d))
    s1y = [(net.send(s1.at[y], s1.at[y], dev(dy=d)), d) for d in range(1, NY)]

    dnx = []
    for d in (1, 3, 2):
        dnx.append((net.send(down.at[my_half], DN.at[x, my_half], dev(dx=d)), d))

    own_g.wait()
    own_u.wait()
    for i, W, d in gux:
        net.arrive(i, wslice(W, md(x - d, NX), y, c), dev(dx=-d))

    def wblock(W, yb, cc):
        return W.at[:, pl.ds(pl.multiple_of((yb * 2 + cc) * rows, 8), rows)]

    mats = (G, U)
    to_partner = []

    def share(k, yb):
        for W in mats:
            region = wblock(W, yb, c)
            to_partner.append((net.send(region, region, partner), W, yb))

    def wring_send(s):
        fwd, bwd = md(y - (s - 1), NY), md(y + (s - 1), NY)
        ids = []
        for m, W in enumerate(mats):
            if s < 4 or m == 0:
                ids.append((net.send(wblock(W, fwd, c), wblock(W, fwd, c), dev(dy=1)), W, md(y - s, NY), -1))
            if s < 4 or m == 1:
                ids.append((net.send(wblock(W, bwd, c), wblock(W, bwd, c), dev(dy=-1)), W, md(y + s, NY), 1))
        return ids

    def wring_arrive(ids):
        for i, W, yb, side in ids:
            net.arrive(i, wblock(W, yb, c), dev(dy=side))

    w_ids = wring_send(1)
    share(0, y)

    nt = F // 256

    def permute(j, carry):
        cols = pl.ds(pl.multiple_of(j * 256, 256), 256)
        onehot = lax.broadcasted_iota(jnp.int32, (F, 256), 0) == kperm[:, cols]
        aperm[:, cols] = jnp.dot(
            att[...], jnp.where(onehot, 1.0, 0.0).astype(bf16), preferred_element_type=f32
        ).astype(bf16)
        return carry

    lax.fori_loop(0, nt, permute, 0)

    for i, d in s1y:
        net.arrive(i, s1.at[md(y - d, NY)], dev(dy=-d))
    for yb in range(NY):
        for xb in range(NX):
            at = (yb * NX + xb) * 3
            s1f[at : at + 3, :] = s1[yb, xb].astype(f32)

    own_rows = NY * NX * 3

    def oblock(zb, cc, lo=0, n=own_rows):
        return OW.at[pl.ds(pl.multiple_of((zb * 2 + cc) * own_rows + lo, 8), n)]

    OW[pl.ds(pl.multiple_of((z * 2 + c) * own_rows, 8), own_rows), :] = s1f[...].astype(bf16)

    o_partner = []

    def oshare(zb):
        o_partner.append((net.send(oblock(zb, c), oblock(zb, c), partner), zb))

    def oring_send(s):
        fwd, bwd = md(z - (s - 1), NZ), md(z + (s - 1), NZ)
        lo, n = ((0, own_rows), (0, own_rows)) if s < 4 else ((0, own_rows // 2), (own_rows // 2, own_rows // 2)), None
        (flo, fn), (blo, bn) = lo
        a = net.send(oblock(fwd, c, flo, fn), oblock(fwd, c, flo, fn), dev(dz=1))
        b = net.send(oblock(bwd, c, blo, bn), oblock(bwd, c, blo, bn), dev(dz=-1))
        return [
            (a, oblock(md(z - s, NZ), c, flo, fn), -1),
            (b, oblock(md(z + s, NZ), c, blo, bn), 1),
        ]

    def ring_arrive(ids):
        for i, region, side in ids:
            net.arrive(i, region, dev(dz=side))

    o_ids = oring_send(1)
    oshare(z)
    ring_arrive(o_ids)
    o_ids = oring_send(2)
    oshare(md(z - 1, NZ))
    oshare(md(z + 1, NZ))
    ring_arrive(o_ids)
    o_ids = oring_send(3)
    oshare(md(z - 2, NZ))
    oshare(md(z + 2, NZ))

    wring_arrive(w_ids)
    w_ids = wring_send(2)
    share(1, md(y - 1, NY))
    share(2, md(y + 1, NY))

    ring_arrive(o_ids)
    o_ids = oring_send(4)
    oshare(md(z - 3, NZ))
    oshare(md(z + 3, NZ))

    dn_partner = []
    own_d.wait()
    for i, d in dnx:
        region = DN.at[md(x - d, NX), my_half]
        net.arrive(i, region, dev(dx=-d))
        dn_partner.append((net.send(region, region, partner), d))

    ring_arrive(o_ids)
    oshare(md(z - 4, NZ))
    for i, zb in o_partner:
        net.arrive(i, oblock(zb, 1 - c), partner)

    def project(j, carry):
        cols = pl.ds(pl.multiple_of(j * 256, 256), 256)
        acc = jnp.dot(aperm[...], OW[:, cols], preferred_element_type=f32)
        tok[0, :, cols] = (res[:, cols].astype(f32) + acc).astype(bf16)
        return carry

    lax.fori_loop(0, nt, project, 0)

    def tring_send(s):
        src_f, dst_f = rel_slot(-(s - 1)), rel_slot(-s)
        src_b, dst_b = rel_slot(s - 1), rel_slot(s)
        if s < 4:
            a = net.send(tok.at[src_f], tok.at[dst_f], dev(dz=1))
            b = net.send(tok.at[src_b], tok.at[dst_b], dev(dz=-1))
            return [(a, tok.at[dst_f], -1), (b, tok.at[dst_b], 1)]
        lo, hi = pl.ds(0, T // 2), pl.ds(T // 2, T // 2)
        a = net.send(tok.at[src_f, lo], tok.at[dst_f, lo], dev(dz=1))
        b = net.send(tok.at[src_b, hi], tok.at[dst_b, hi], dev(dz=-1))
        return [(a, tok.at[dst_f, lo], -1), (b, tok.at[dst_b, hi], 1)]

    for i, d in metas:
        net.arrive(i, meta.at[rel_slot(-d)], dev(dz=-d))

    def select(p):
        row = lax.broadcasted_iota(jnp.int32, (PAIR, T), 0).astype(f32)
        for e in range(NX):
            ma = meta[2 * p, e : e + 1, :] == row
            mb = meta[2 * p + 1, e : e + 1, :] + float(CAP) == row
            wa = jnp.where(ma, meta[2 * p, 4 + e : 5 + e, :], 0.0)
            wb = jnp.where(mb, meta[2 * p + 1, 4 + e : 5 + e, :], 0.0)
            sel[p, e, :, 0:T] = jnp.where(ma, 1.0, 0.0).astype(bf16)
            sel[p, e, :, T : 2 * T] = jnp.where(mb, 1.0, 0.0).astype(bf16)
            w = jnp.sum(wa + wb, axis=1, keepdims=True)
            wrow[p, e] = jnp.broadcast_to(w, (PAIR, 128))

    def gather(p, q):
        both = sel[p].reshape(NX * PAIR, 2 * T)

        def tile(j, carry):
            cols = pl.ds(pl.multiple_of(j * 256, 256), 256)
            v = jnp.dot(both, tok[2 * p : 2 * p + 2, :, cols].reshape(2 * T, 256), preferred_element_type=f32)
            X[:, q * PAIR : (q + 1) * PAIR, cols] = v.astype(bf16).reshape(NX, PAIR, 256)
            return carry

        lax.fori_loop(0, nt, tile, 0)

    def experts(pairs):
        def one(e, carry):
            xe = X[e]
            g = jnp.dot(xe, G[e], preferred_element_type=f32)
            u = jnp.dot(xe, U[e], preferred_element_type=f32)
            h = (jax.nn.silu(g) * u).astype(bf16)
            for j in range(F // 512):
                o = jnp.dot(h, DN[e, :, j * 512 : (j + 1) * 512], preferred_element_type=f32)
                for q, p in enumerate(pairs):
                    w = wrow[p, e][:, 0:1]
                    Y[p, e, :, j * 512 : (j + 1) * 512] = (
                        o[q * PAIR : (q + 1) * PAIR, :] * w
                    ).astype(bf16)
            return carry

        lax.fori_loop(0, NX, one, 0)

    t_ids = tring_send(1)
    for p in range(4):
        select(p)

    wring_arrive(w_ids)
    w_ids = wring_send(3)
    share(3, md(y - 2, NY))
    share(4, md(y + 2, NY))

    ring_arrive(t_ids)
    t_ids = tring_send(2)
    gather(1, 0)
    ring_arrive(t_ids)
    t_ids = tring_send(3)
    gather(2, 1)

    wring_arrive(w_ids)
    w_ids = wring_send(4)
    share(5, md(y - 3, NY))
    share(6, md(y + 3, NY))
    ring_arrive(t_ids)
    t_ids = tring_send(4)
    wring_arrive(w_ids)
    share(7, md(y - 4, NY))
    for i, d in dn_partner:
        net.arrive(i, DN.at[md(x - d, NX), pl.ds(pl.multiple_of((1 - c) * half, 8), half)], partner)
    for i, W, yb in to_partner:
        net.arrive(i, wblock(W, yb, 1 - c), partner)

    experts((1, 2))
    gather(3, 0)
    ring_arrive(t_ids)
    gather(0, 1)
    experts((3, 0))

    def mix(slot, b):
        p, h = slot // 2, slot % 2

        def tile(j, carry):
            cols = pl.ds(pl.multiple_of(j * 256, 256), 256)
            part[b, :, cols] = lax.dot_general(
                sel[p, :, :, h * T : (h + 1) * T].reshape(NX * PAIR, T),
                Y[p, :, :, cols].reshape(NX * PAIR, 256),
                (((0,), (0,)), ((), ())),
                preferred_element_type=f32,
            )
            return carry

        lax.fori_loop(0, nt, tile, 0)

    lo, hi = pl.ds(0, T // 2), pl.ds(T // 2, T // 2)
    mix(rel_slot(4), 0)
    SB[0, 0, lo] = part[0, lo].astype(bf16)
    SB[1, 0, hi] = part[0, hi].astype(bf16)
    r_ids = [
        (net.send(SB.at[0, 0, lo], RB.at[0, 0, lo], dev(dz=1)), RB.at[0, 0, lo], -1),
        (net.send(SB.at[1, 0, hi], RB.at[1, 0, hi], dev(dz=-1)), RB.at[1, 0, hi], 1),
    ]
    for s in (2, 3, 4):
        r = 5 - s
        mix(rel_slot(r), 0)
        mix(rel_slot(-r), 1)
        ring_arrive(r_ids)
        r_ids = []
        for b, (side, got) in enumerate(((1, lo), (-1, hi))):
            if s == 2:
                keep = hi if b == 0 else lo
                SB[b, s - 1, keep] = part[b, keep].astype(bf16)
                SB[b, s - 1, got] = (part[b, got] + RB[b, 0, got].astype(f32)).astype(bf16)
            else:
                SB[b, s - 1] = (part[b] + RB[b, s - 2].astype(f32)).astype(bf16)
            r_ids.append((net.send(SB.at[b, s - 1], RB.at[b, s - 1], dev(dz=side)), RB.at[b, s - 1], -side))
    mix(0, 0)
    ring_arrive(r_ids)
    total = tok[0].astype(f32) + (part[0] + RB[0, 3].astype(f32) + RB[1, 3].astype(f32))
    scale = lax.rsqrt(jnp.mean(total * total, axis=1, keepdims=True) + 1e-06)
    out[...] = (total * scale * gain[...]).astype(bf16)
    net.drain()
    assert net.count <= N_COPIES


def row_order():
    z, c, y, x, j = np.meshgrid(
        np.arange(NZ), np.arange(2), np.arange(NY), np.arange(NX), np.arange(3), indexing="ij"
    )
    return (((y * 2 + c) * NX + x) * NZ + z).reshape(-1) * 3 + j.reshape(-1)


def body(attention, residual, out_weight, gate_weight, up_weight, down_weight, routes, router_scores, norm_gain):
    T, F = attention.shape
    rows, H = gate_weight.shape[1:]
    kperm = jnp.asarray(row_order()[None, :], jnp.int32)
    bf16, f32 = jnp.bfloat16, jnp.float32
    vm = pl.BlockSpec(memory_space=pltpu.VMEM)
    hbm = pl.BlockSpec(memory_space=pl.ANY)
    return pl.pallas_call(
        kernel,
        out_shape=jax.ShapeDtypeStruct((T, F), bf16),
        in_specs=[vm, vm, vm, hbm, hbm, hbm, vm, vm, vm, vm],
        out_specs=vm,
        scratch_shapes=[
            pltpu.VMEM((NY, NX, 3, F), bf16),
            pltpu.VMEM((NY * NX * 3, F), f32),
            pltpu.VMEM((F, F), bf16),
            pltpu.VMEM((NX, F, H), bf16),
            pltpu.VMEM((NX, F, H), bf16),
            pltpu.VMEM((NX, H, F), bf16),
            pltpu.VMEM((NZ, T, F), bf16),
            pltpu.VMEM((NZ, 8, T), f32),
            pltpu.VMEM((NZ, 8, T), f32),
            pltpu.VMEM((4, NX, PAIR, 2 * T), bf16),
            pltpu.VMEM((4, NX, PAIR, 128), f32),
            pltpu.VMEM((NX, 2 * PAIR, F), bf16),
            pltpu.VMEM((4, NX, PAIR, F), bf16),
            pltpu.VMEM((2, 4, T, F), bf16),
            pltpu.VMEM((2, 4, T, F), bf16),
            pltpu.VMEM((2, T, F), f32),
            pltpu.VMEM((T, F), bf16),
            pltpu.SemaphoreType.DMA((N_COPIES,)),
            pltpu.SemaphoreType.DMA((N_COPIES,)),
            pltpu.SemaphoreType.DMA((4,)),
        ],
        compiler_params=pltpu.CompilerParams(
            collective_id=0, has_side_effects=True, vmem_limit_bytes=62 * 1024 * 1024
        ),
    )(
        attention, residual, out_weight, gate_weight[0], up_weight[0], down_weight[0],
        routes.T, router_scores.T, norm_gain[None, :], kperm,
    )


def solution(mesh):
    rows = P(("dp", "expert"), None)
    in_specs = (
        rows, rows, rows, P("expert", "dp", None), P("expert", "dp", None), P("expert", None, None),
        rows, rows, P(),
    )
    return jax.shard_map(body, mesh=mesh, in_specs=in_specs, out_specs=rows, check_vma=False)
```

```python
import jax
import jax.numpy as jnp
import numpy as np
from jax import lax
from jax.experimental import pallas as pl
from jax.experimental.pallas import tpu as pltpu
from jax.sharding import PartitionSpec as P

NX, NY, NZ = 4, 8, 8
CAP = 40
PAIR = 2 * CAP
SLOT = {0: 0, 4: 1, 1: 2, -1: 3, 2: 4, -2: 5, 3: 6, -3: 7}


def rel_slot(r):
    r = r % NZ
    return SLOT[r if r <= 4 else r - NZ]


class Net:
    def __init__(self, send_sems, recv_sems):
        self.ss, self.rs, self.count, self.sent = send_sems, recv_sems, 0, []

    def send(self, src, dst, device):
        i = self.count
        self.count += 1
        copy = pltpu.make_async_remote_copy(
            src_ref=src, dst_ref=dst, send_sem=self.ss.at[i], recv_sem=self.rs.at[i],
            device_id=device, device_id_type=pl.DeviceIdType.MESH,
        )
        copy.start()
        self.sent.append(copy)
        return i

    def arrive(self, i, region, device):
        pltpu.make_async_remote_copy(
            src_ref=region, dst_ref=region, send_sem=self.ss.at[i], recv_sem=self.rs.at[i],
            device_id=device, device_id_type=pl.DeviceIdType.MESH,
        ).wait_recv()

    def drain(self):
        for copy in self.sent:
            copy.wait_send()


N_COPIES = 176
NEAR = 1024


class Ring:
    def __init__(self, net, plus, minus, region, halves, split, relative=False):
        self.net, self.plus, self.minus = net, plus, minus
        self.region, self.halves, self.split, self.relative = region, halves, split, relative
        self.flight = {}

    def parts(self, s):
        lo, hi = self.halves
        if s == 4:
            return [(1, lo), (-1, hi)]
        if self.split:
            return [(1, lo), (-1, hi), (1, hi), (-1, lo)]
        return [(1, None), (-1, None)]

    def push(self, s, way, half):
        ref = self.region(way * (s - 1), half)
        dst = self.region(way * s, half) if self.relative else ref
        i = self.net.send(ref, dst, self.plus if way > 0 else self.minus)
        self.flight.setdefault(s, []).append((i, way, half))

    def start(self):
        for way, half in self.parts(1):
            self.push(1, way, half)

    def advance(self, s):
        for i, way, half in self.flight[s]:
            self.net.arrive(i, self.region(way * s, half), self.minus if way > 0 else self.plus)
            if s < 4:
                for way2, half2 in self.parts(s + 1):
                    if way2 == way and (half is None or half2 == half):
                        self.push(s + 1, way, half2)


def kernel(
    att, res, ow, gate, up, down, routes_t, scores_t, gain, kperm,
    out,
    s1a, s1c, s1f, OWA, OWC, GU, DN, tok, meta, tab, sel, wrow, X, Y, SB, RB, part, aperm,
    send_sems, recv_sems, loc_sems,
):
    f32, bf16 = jnp.float32, jnp.bfloat16
    T, F = att.shape
    rows, H = gate.shape
    KEEP = H + H // 2
    dp, ex = lax.axis_index("dp"), lax.axis_index("expert")
    y, c = lax.div(dp, 2), lax.rem(dp, 2)
    x, z = lax.div(ex, NZ), lax.rem(ex, NZ)

    def md(a, n):
        return lax.rem(a + 2 * n, n)

    def dev(dx=0, dy=0, dz=0, other=False):
        cc = 1 - c if other else c
        return (md(y + dy, NY) * 2 + cc, md(x + dx, NX) * NZ + md(z + dz, NZ))

    partner = dev(other=True)
    net = Net(send_sems, recv_sems)

    def local(k, src, dst):
        copy = pltpu.make_async_copy(src, dst, loc_sems.at[k])
        copy.start()
        return copy

    own_a = local(0, ow.at[:, 0:NEAR], s1a.at[x, y])
    own_c = local(1, ow.at[:, NEAR:F], s1c.at[x, z])
    own_g = local(2, gate, GU.at[x, y, c, :, 0:H])
    own_u = local(3, up, GU.at[x, y, c, :, H : 2 * H])
    own_d = local(4, down, DN.at[x])

    barrier = pltpu.get_barrier_semaphore()
    peers = (
        [dev(dx=d) for d in range(1, NX)] + [dev(dy=d) for d in range(1, NY)]
        + [dev(dz=d) for d in range(1, NZ)] + [partner]
    )
    for p in peers:
        pl.semaphore_signal(barrier, inc=1, device_id=p, device_id_type=pl.DeviceIdType.MESH)

    r8 = lax.broadcasted_iota(jnp.int32, (NZ * 8, T), 0)
    expert_of = (r8 % 4) * NZ + r8 // 8
    scores = scores_t[...]
    combine = scores / jnp.sum(scores, axis=0, keepdims=True)
    member = jnp.zeros((NZ * 8, T), f32)
    weight = jnp.zeros((NZ * 8, T), f32)
    for k in range(routes_t.shape[0]):
        hit = routes_t[k : k + 1, :] == expert_of
        member = member + jnp.where(hit, 1.0, 0.0)
        weight = weight + jnp.where(hit, combine[k : k + 1, :], 0.0)
    before = lax.broadcasted_iota(jnp.int32, (T, T), 0) < lax.broadcasted_iota(jnp.int32, (T, T), 1)
    place = jnp.dot(member.astype(bf16), jnp.where(before, 1.0, 0.0).astype(bf16), preferred_element_type=f32)
    table = jnp.where(r8 % 8 < 4, jnp.where(member > 0.5, place, -1000.0), weight)
    tab[...] = table.reshape(NZ, 8, T)
    meta[0] = tab[z]

    nt = F // 256

    def permute(n):
        def tile(j, carry):
            cols = pl.ds(pl.multiple_of(j * 256, 256), 256)
            onehot = lax.broadcasted_iota(jnp.int32, (F, 256), 0) == kperm[n : n + 1, cols]
            aperm[n, :, cols] = jnp.dot(
                att[...], jnp.where(onehot, 1.0, 0.0).astype(bf16), preferred_element_type=f32
            ).astype(bf16)
            return carry

        lax.fori_loop(0, nt, tile, 0)

    permute(0)
    permute(1)
    pl.semaphore_wait(barrier, len(peers))

    far_first = (4, 3, 5, 2, 6, 1, 7)
    a1 = [(net.send(ow.at[:, 0:NEAR], s1a.at[x, y], dev(dy=d)), d) for d in far_first]
    c1 = [(net.send(ow.at[:, NEAR:F], s1c.at[x, z], dev(dz=d)), d) for d in far_first]

    blk_lo, blk_hi = pl.ds(0, rows // 2), pl.ds(rows // 2, rows // 2)
    full = pl.ds(0, rows)

    def block(e, half=None):
        return GU.at[e, y, c, full if half is None else half, 0:KEEP]

    def piece(e):
        return Ring(
            net, dev(dy=1), dev(dy=-1),
            lambda k, half: GU.at[e, md(y - k, NY), c, full if half is None else half, 0:KEEP],
            (blk_lo, blk_hi), False,
        )

    order = (x, md(x - 1, NX), md(x + 1, NX), md(x + 2, NX))
    pieces = [piece(e) for e in order]
    late = Ring(
        net, dev(dy=1), dev(dy=-1),
        lambda k, half: GU.at[x, md(y - k, NY), c, full if half is None else half, KEEP : 2 * H],
        (blk_lo, blk_hi), False,
    )
    own_g.wait()
    own_u.wait()
    wx = [net.send(block(x), block(x), dev(dx=1)), net.send(block(x), block(x), dev(dx=-1))]
    late.start()
    pieces[0].start()

    own_a.wait()
    for i, d in a1:
        net.arrive(i, s1a.at[x, md(y - d, NY)], dev(dy=-d))
    a2 = [(net.send(s1a.at[x], s1a.at[x], dev(dx=d)), d) for d in (2, 1, 3)]
    own_c.wait()
    for i, d in c1:
        net.arrive(i, s1c.at[x, md(z - d, NZ)], dev(dz=-d))
    c2 = [(net.send(s1c.at[x], s1c.at[x], dev(dx=d)), d) for d in (2, 1, 3)]
    metas = []
    for d in range(1, NZ):
        metas.append((net.send(tab.at[md(z + d, NZ)], meta.at[rel_slot(-d)], dev(dz=d)), d))

    late.advance(1)
    net.arrive(wx[0], block(order[1]), dev(dx=-1))
    net.arrive(wx[1], block(order[2]), dev(dx=1))
    wx2 = [
        net.send(block(order[1], blk_lo), block(order[1], blk_lo), dev(dx=1)),
        net.send(block(order[2], blk_hi), block(order[2], blk_hi), dev(dx=-1)),
    ]
    pieces[1].start()
    late.advance(2)
    late.advance(3)

    own_rows = NY * NX * 3

    def orows(b, cc, half):
        lo, n = (0, own_rows) if half is None else half
        return pl.ds(pl.multiple_of((b * 2 + cc) * own_rows + lo, 8), n)

    ohalves = ((0, own_rows // 2), (own_rows // 2, own_rows // 2))
    ring_a = Ring(
        net, dev(dz=1), dev(dz=-1), lambda k, half: OWA.at[orows(md(z - k, NZ), c, half)], ohalves, True
    )
    ring_c = Ring(
        net, dev(dy=1), dev(dy=-1), lambda k, half: OWC.at[orows(md(y - k, NY), c, half)], ohalves, False
    )

    def collect(s1, dst, b, lo, n):
        for xb in range(NX):
            for q in range(8):
                at = (xb * 8 + q) * 3
                s1f[at : at + 3, lo : lo + n] = s1[xb, q].astype(f32)
        dst[orows(b, c, None), :] = s1f[:, lo : lo + n].astype(bf16)

    o_partner = []

    def oshare(dst, b):
        ref = dst.at[orows(b, c, None)]
        o_partner.append((net.send(ref, ref, partner), dst, b))

    def ashare(s):
        for k in ((s, -s) if 0 < s < 4 else (s,)):
            oshare(OWA, md(z - k, NZ))

    def cshare(s):
        for k in ((s, -s) if 0 < s < 4 else (s,)):
            oshare(OWC, md(y - k, NY))

    for i, d in a2:
        net.arrive(i, s1a.at[md(x - d, NX)], dev(dx=-d))
    collect(s1a, OWA, z, 0, NEAR)
    ring_a.start()
    for i, d in c2:
        net.arrive(i, s1c.at[md(x - d, NX)], dev(dx=-d))
    collect(s1c, OWC, y, NEAR, F - NEAR)
    ring_c.start()
    pieces[2].start()
    ashare(0)
    cshare(0)

    late.advance(4)
    w_partner = [[], [], [], []]

    def lates(e, lo=0, n=NY, cc=None):
        return GU.at[e, pl.ds(lo, n), c if cc is None else cc, :, KEEP : 2 * H]

    def late_share(n):
        e = order[n]
        w_partner[n].append((net.send(lates(e), lates(e), partner), lates(e, cc=1 - c)))

    lx = [net.send(lates(x), lates(x), dev(dx=1)), net.send(lates(x), lates(x), dev(dx=-1))]
    late_share(0)
    half = H // 2

    def drows(e, lo=0, n=half, cc=None):
        return DN.at[e, pl.ds(pl.multiple_of((c if cc is None else cc) * half + lo, 8), n)]

    my_down = down.at[pl.ds(pl.multiple_of(c * half, 8), half)]
    dx = [net.send(my_down, drows(x), dev(dx=1)), net.send(my_down, drows(x), dev(dx=-1))]

    def down_share(n):
        e = order[n]
        w_partner[n].append((net.send(drows(e), drows(e), partner), drows(e, cc=1 - c)))

    net.arrive(wx2[0], block(order[3], blk_lo), dev(dx=-1))
    net.arrive(wx2[1], block(order[3], blk_hi), dev(dx=1))

    def gshare(s):
        for k in ((s, -s) if s else (0,)):
            yb = md(y - k, NY)
            ref = GU.at[:, yb, c, :, 0:KEEP]
            g_partner.append((net.send(ref, ref, partner), GU.at[:, yb, 1 - c, :, 0:KEEP]))

    g_partner = []
    ring_c.advance(1)
    pieces[3].start()
    gshare(0)
    ring_a.advance(1)
    cshare(1)
    ashare(1)
    ring_c.advance(2)
    pieces[0].advance(1)
    ring_a.advance(2)
    cshare(2)
    ashare(2)
    net.arrive(lx[0], lates(order[1]), dev(dx=-1))
    net.arrive(lx[1], lates(order[2]), dev(dx=1))
    lx2 = [
        net.send(lates(order[1], 0, NY // 2), lates(order[1], 0, NY // 2), dev(dx=1)),
        net.send(lates(order[2], NY // 2, NY // 2), lates(order[2], NY // 2, NY // 2), dev(dx=-1)),
    ]
    late_share(1)
    late_share(2)
    ring_c.advance(3)
    ring_a.advance(3)
    for n in (1, 2, 3):
        pieces[n].advance(1)
    cshare(3)
    ashare(3)
    ring_c.advance(4)
    cshare(4)
    ring_a.advance(4)
    ashare(4)
    gshare(1)
    for i, dst, b in o_partner:
        net.arrive(i, dst.at[orows(b, 1 - c, None)], partner)

    def project(W, n, lo, tiles):
        def tile(j, carry):
            cols = pl.ds(pl.multiple_of(j * 256, 256), 256)
            to = pl.ds(pl.multiple_of(lo + j * 256, 256), 256)
            acc = jnp.dot(aperm[n], W[:, cols], preferred_element_type=f32)
            tok[0, :, to] = (res[:, to].astype(f32) + acc).astype(bf16)
            return carry

        lax.fori_loop(0, tiles, tile, 0)

    project(OWA, 0, 0, NEAR // 256)
    project(OWC, 1, NEAR, (F - NEAR) // 256)

    tlo, thi = pl.ds(0, T // 2), pl.ds(T // 2, T // 2)
    ring_t = Ring(
        net, dev(dz=1), dev(dz=-1), lambda k, half: tok.at[rel_slot(-k), half], (tlo, thi), True, True
    )
    ring_t.start()
    for i, d in metas:
        net.arrive(i, meta.at[rel_slot(-d)], dev(dz=-d))

    def select(p):
        row = lax.broadcasted_iota(jnp.int32, (PAIR, T), 0).astype(f32)
        for e in range(NX):
            ma = meta[2 * p, e : e + 1, :] == row
            mb = meta[2 * p + 1, e : e + 1, :] + float(CAP) == row
            wa = jnp.where(ma, meta[2 * p, 4 + e : 5 + e, :], 0.0)
            wb = jnp.where(mb, meta[2 * p + 1, 4 + e : 5 + e, :], 0.0)
            sel[p, e, :, 0:T] = jnp.where(ma, 1.0, 0.0).astype(bf16)
            sel[p, e, :, T : 2 * T] = jnp.where(mb, 1.0, 0.0).astype(bf16)
            w = jnp.sum(wa + wb, axis=1, keepdims=True)
            wrow[p, e] = jnp.broadcast_to(w, (PAIR, 128))

    def gather(p, q):
        both = sel[p].reshape(NX * PAIR, 2 * T)

        def tile(j, carry):
            cols = pl.ds(pl.multiple_of(j * 256, 256), 256)
            v = jnp.dot(both, tok[2 * p : 2 * p + 2, :, cols].reshape(2 * T, 256), preferred_element_type=f32)
            X[:, q * PAIR : (q + 1) * PAIR, cols] = v.astype(bf16).reshape(NX, PAIR, 256)
            return carry

        lax.fori_loop(0, nt, tile, 0)

    def expert(pairs, e):
        gu = jnp.dot(X[e], GU[e].reshape(F, 2 * H), preferred_element_type=f32)
        h = (jax.nn.silu(gu[:, 0:H]) * gu[:, H : 2 * H]).astype(bf16)
        for j in range(F // 512):
            o = jnp.dot(h, DN[e, :, j * 512 : (j + 1) * 512], preferred_element_type=f32)
            for q, p in enumerate(pairs):
                w = wrow[p, e][:, 0:1]
                Y[p, e, :, j * 512 : (j + 1) * 512] = (o[q * PAIR : (q + 1) * PAIR, :] * w).astype(bf16)

    for p in range(4):
        select(p)
    for ring in pieces:
        ring.advance(2)
    gshare(2)
    own_d.wait()
    net.arrive(dx[0], drows(order[1]), dev(dx=-1))
    net.arrive(dx[1], drows(order[2]), dev(dx=1))
    dx2 = [
        net.send(drows(order[1], 0, half // 2), drows(order[1], 0, half // 2), dev(dx=1)),
        net.send(drows(order[2], half // 2, half // 2), drows(order[2], half // 2, half // 2), dev(dx=-1)),
    ]
    down_share(1)
    down_share(2)
    ring_t.advance(1)
    net.arrive(lx2[0], lates(order[3], 0, NY // 2), dev(dx=-1))
    net.arrive(lx2[1], lates(order[3], NY // 2, NY // 2), dev(dx=1))
    late_share(3)
    for ring in pieces:
        ring.advance(3)
    gshare(3)
    ring_t.advance(2)
    net.arrive(dx2[0], drows(order[3], 0, half // 2), dev(dx=-1))
    net.arrive(dx2[1], drows(order[3], half // 2, half // 2), dev(dx=1))
    down_share(3)
    for n, ring in enumerate(pieces):
        ring.advance(4)
        far = md(y - 4, NY)
        ref = GU.at[order[n], far, c, :, 0:KEEP]
        w_partner[n].append((net.send(ref, ref, partner), GU.at[order[n], far, 1 - c, :, 0:KEEP]))
    ring_t.advance(3)
    gather(3, 0)
    ring_t.advance(4)
    gather(0, 1)
    for i, ref in g_partner:
        net.arrive(i, ref, partner)
    for n in range(NX):
        for i, ref in w_partner[n]:
            net.arrive(i, ref, partner)
        expert((3, 0), order[n])

    def mix(slot, b):
        p, h = slot // 2, slot % 2

        def tile(j, carry):
            cols = pl.ds(pl.multiple_of(j * 256, 256), 256)
            part[b, :, cols] = lax.dot_general(
                sel[p, :, :, h * T : (h + 1) * T].reshape(NX * PAIR, T),
                Y[p, :, :, cols].reshape(NX * PAIR, 256),
                (((0,), (0,)), ((), ())),
                preferred_element_type=f32,
            )
            return carry

        lax.fori_loop(0, nt, tile, 0)

    def rsend(s, b, half):
        i = net.send(SB.at[b, s - 1, half], RB.at[b, s - 1, half], dev(dz=1 if b == 0 else -1))
        return (i, b, half)

    def rarrive(s, flight):
        i, b, half = flight
        net.arrive(i, RB.at[b, s - 1, half], dev(dz=-1 if b == 0 else 1))

    mix(rel_slot(4), 0)
    r_ids = []
    for b, half in ((0, tlo), (1, thi)):
        SB[b, 0, half] = part[0, half].astype(bf16)
        r_ids.append(rsend(1, b, half))
    mix(rel_slot(3), 0)
    mix(rel_slot(-3), 1)
    new = []
    for b, half in ((0, thi), (1, tlo)):
        SB[b, 1, half] = part[b, half].astype(bf16)
        new.append(rsend(2, b, half))
    gather(1, 0)
    gather(2, 1)

    def one(e, carry):
        expert((1, 2), e)
        return carry

    lax.fori_loop(0, NX, one, 0)
    for s in (2, 3, 4):
        if s > 2:
            r = 5 - s
            mix(rel_slot(r), 0)
            mix(rel_slot(-r), 1)
            new = []
        for flight in r_ids:
            _, b, half = flight
            rarrive(s - 1, flight)
            SB[b, s - 1, half] = (part[b, half] + RB[b, s - 2, half].astype(f32)).astype(bf16)
            new.append(rsend(s, b, half))
        r_ids = new
    mix(0, 0)
    for flight in r_ids:
        rarrive(4, flight)
    total = tok[0].astype(f32) + (part[0] + RB[0, 3].astype(f32) + RB[1, 3].astype(f32))
    scale = lax.rsqrt(jnp.mean(total * total, axis=1, keepdims=True) + 1e-06)
    out[...] = (total * scale * gain[...]).astype(bf16)
    net.drain()
    assert net.count <= N_COPIES


def row_order():
    def order(*axes):
        g = dict(zip(axes, np.meshgrid(*[np.arange(SIZE[a]) for a in axes], indexing="ij")))
        return ((((g["y"] * 2 + g["c"]) * NX + g["x"]) * NZ + g["z"]) * 3 + g["j"]).reshape(-1)

    return np.stack([order("z", "c", "x", "y", "j"), order("y", "c", "x", "z", "j")])


SIZE = {"x": NX, "y": NY, "z": NZ, "c": 2, "j": 3}


def body(attention, residual, out_weight, gate_weight, up_weight, down_weight, routes, router_scores, norm_gain):
    T, F = attention.shape
    rows, H = gate_weight.shape[1:]
    kperm = jnp.asarray(row_order(), jnp.int32)
    bf16, f32 = jnp.bfloat16, jnp.float32
    vm = pl.BlockSpec(memory_space=pltpu.VMEM)
    hbm = pl.BlockSpec(memory_space=pl.ANY)
    return pl.pallas_call(
        kernel,
        out_shape=jax.ShapeDtypeStruct((T, F), bf16),
        in_specs=[vm, vm, vm, hbm, hbm, hbm, vm, vm, vm, vm],
        out_specs=vm,
        scratch_shapes=[
            pltpu.VMEM((NX, NY, 3, NEAR), bf16),
            pltpu.VMEM((NX, NZ, 3, F - NEAR), bf16),
            pltpu.VMEM((NY * NX * 3, F), f32),
            pltpu.VMEM((F, NEAR), bf16),
            pltpu.VMEM((F, F - NEAR), bf16),
            pltpu.VMEM((NX, NY, 2, rows, 2 * H), bf16),
            pltpu.VMEM((NX, H, F), bf16),
            pltpu.VMEM((NZ, T, F), bf16),
            pltpu.VMEM((NZ, 8, T), f32),
            pltpu.VMEM((NZ, 8, T), f32),
            pltpu.VMEM((4, NX, PAIR, 2 * T), bf16),
            pltpu.VMEM((4, NX, PAIR, 128), f32),
            pltpu.VMEM((NX, 2 * PAIR, F), bf16),
            pltpu.VMEM((4, NX, PAIR, F), bf16),
            pltpu.VMEM((2, 4, T, F), bf16),
            pltpu.VMEM((2, 4, T, F), bf16),
            pltpu.VMEM((2, T, F), f32),
            pltpu.VMEM((2, T, F), bf16),
            pltpu.SemaphoreType.DMA((N_COPIES,)),
            pltpu.SemaphoreType.DMA((N_COPIES,)),
            pltpu.SemaphoreType.DMA((5,)),
        ],
        compiler_params=pltpu.CompilerParams(
            collective_id=0, has_side_effects=True, vmem_limit_bytes=62 * 1024 * 1024
        ),
    )(
        attention, residual, out_weight, gate_weight[0], up_weight[0], down_weight[0],
        routes.T, router_scores.T, norm_gain[None, :], kperm,
    )


def solution(mesh):
    rows = P(("dp", "expert"), None)
    in_specs = (
        rows, rows, rows, P("expert", "dp", None), P("expert", "dp", None), P("expert", None, None),
        rows, rows, P(),
    )
    return jax.shard_map(body, mesh=mesh, in_specs=in_specs, out_specs=rows, check_vma=False)
```
